32 devices in a mesh: dp: 4 (over y, core), fsdp: 8 (over z, x).
Axes of the slice: x: 2, y: 2, z: 4, core: 2. Of those that a mesh axis runs over, the one named last changes fastest.
Arguments:
- hidden_in: bfloat16 [2, 32, 1024, 576], P(None, ('dp', 'fsdp')), may hold values from -0.59765625 to 0.59765625
- seg_ids: int32 [2, 32, 1024], P(None, ('dp', 'fsdp')), may hold values from 0 to 7, never falling along the last dimension, each value on 1 to 512 neighbouring positions
- out_grad: bfloat16 [2, 32, 1024, 576], P(None, ('dp', 'fsdp')), may hold values from -6 to 6
- gains: float32 [2, 576], P(None, 'fsdp'), may hold values from 0.5 to 1.5
- matrices: float32 [576, 6144], P('fsdp'), may hold values from -8 to 8
- gain_momentum: float32 [2, 576], P(None, 'fsdp'), may hold values from -0.3 to 0.3
- mat_momentum: float32 [576, 6144], P('fsdp'), may hold values from -0.12 to 0.12
Outputs:
- out_hidden: bfloat16 [2, 32, 1024, 576], P(None, ('dp', 'fsdp'))
- in_grad: float32 [2, 32, 1024, 576], P(None, ('dp', 'fsdp'))
- matrix_grad: float32 [576, 6144], P('fsdp')
- gain_grad: float32 [2, 576], P(None, 'fsdp')
- new_mat_momentum: float32 [576, 6144], P('fsdp')
- new_gain_momentum: float32 [2, 576], P(None, 'fsdp')
- new_matrices: float32 [576, 6144], P('fsdp')
- new_gains: float32 [2, 576], P(None, 'fsdp')
The draws below stay inside these ranges and needn't reach their ends.
Inputs may be any that keep to these rules, and one draw needn't show every extreme that they name: `seg_ids`: within a sequence segment numbers never fall; a document holds at most 512 tokens.
All inputs are finite; a program needn't handle non-finite values.
Results may differ from the reference program's by a relative error of at most 0.01.
The reference program's roundings to bfloat16 on the way count: a program that leaves them out, or rounds other values in their place, can miss the bound.
Values may be sent and summed in bfloat16 or wider, within the bound.
A program may use at most 384 MiB of HBM per device.

```python
import math
import jax
import jax.numpy as jnp
import numpy as np
from jax import lax

D = 576
HEADS = 9
KVH = 3
HD = 64
FF = 1536
MB = 2
SEQ = 1024
NS_STEPS = 5
SEQS = 32
TOKENS = 65536


def draw_matrices(key, part):
    key_list = jax.random.split(key, 6)
    kv_cols = KVH * HD
    query_w = jax.random.normal(key_list[0], (D, D), jnp.float32) / math.sqrt(D)
    key_w = jax.random.normal(key_list[1], (D, kv_cols), jnp.float32) / math.sqrt(D)
    value_w = jax.random.normal(key_list[2], (D, kv_cols), jnp.float32) / math.sqrt(D)
    output_w = jax.random.normal(key_list[3], (D, D), jnp.float32) / math.sqrt(D)
    gate_up = jax.random.normal(key_list[4], (D, 2 * FF), jnp.float32) / math.sqrt(D)
    down_w = jax.random.normal(key_list[5], (D, FF), jnp.float32) / math.sqrt(25 * FF)
    whole = jnp.concatenate([query_w, key_w, value_w, output_w, gate_up, down_w], axis=1)
    return jnp.clip(whole, -8.0, 8.0)


def steps_of(own_key, extent, cuts, smallest, high):
    gain = 1.0
    for dim, shards_of in cuts:
        draws = jax.random.uniform(jax.random.fold_in(jax.random.fold_in(own_key, 6), dim), (shards_of,), jnp.float32, smallest / len(cuts), high / len(cuts))
        gain = gain * jnp.repeat(jnp.exp(draws), extent[dim] // shards_of).reshape((-1,) + (1,) * (len(extent) - 1 - dim))
    return gain


def profile(amount, total, limit, slope):
    weights = [(1 << 20) // math.isqrt(grade ** slope) + 1 for grade in range(2, amount + 1)]
    surplus, holding = total - limit - (amount - 1), [1] * (amount - 1)
    while surplus > 0:
        candidates = [i for i in range(amount - 1) if holding[i] < limit]
        pool, budget = sum([weights[i] for i in candidates]), surplus
        for i in candidates:
            extra = min(limit - holding[i], max(1, budget * weights[i] // pool), surplus)
            holding[i] = holding[i] + extra
            surplus = surplus - extra
    return np.array([limit] + holding)


def ragged_sizes(rng, amount, total, bound, skew):
    if amount == 2:
        one = jax.random.randint(rng, (), max(1, total - bound), min(bound, total - 1) + 1)
        return jnp.stack([one, total - one])
    sizes = jnp.asarray(profile(amount, total, bound, skew), jnp.int32)
    pairs = (amount - 1) // 2
    donor, taker = sizes[1:1 + 2 * pairs:2], sizes[2:2 + 2 * pairs:2]
    margin = jnp.minimum(donor - 1, bound - taker)
    shifted = jax.random.randint(jax.random.fold_in(rng, 1), (pairs,), 0, 1 << 20) % (margin + 1)
    sizes = sizes.at[1:1 + 2 * pairs:2].set(donor - shifted).at[2:2 + 2 * pairs:2].set(taker + shifted)
    return sizes[jax.random.permutation(jax.random.fold_in(rng, 2), amount)]


def scatter_about(key, extent, scale, bound, cuts=(), kind=jnp.bfloat16):
    array = scale * jax.random.normal(key, extent, jnp.float32)
    if cuts:
        array = array * steps_of(key, extent, cuts, -0.22, 0.18)
    return jnp.clip(array, -bound, bound).astype(kind)


def setup_inputs(seed: int = 0) -> dict:
    splits = jax.random.split(jax.random.key(seed), 8)
    return {
        "hidden_in": scatter_about(splits[0], (MB, SEQS, SEQ, D), 0.1, 0.59765625, ((1, 32),)),
        "seg_ids": jax.vmap(lambda own: jnp.searchsorted(jnp.cumsum(ragged_sizes(own, max(4, SEQ // 128), SEQ, SEQ // 2, 2)), jnp.arange(SEQ), side="right"))(jax.random.split(splits[1], MB * SEQS)).reshape((MB, SEQS, SEQ)).astype(jnp.int32),
        "out_grad": scatter_about(splits[2], (MB, SEQS, SEQ, D), 1.0, 6.0, ((1, 32),)),
        "gains": jnp.clip(1.0 + 0.1 * jax.random.normal(splits[3], (2, D), jnp.float32), 0.5, 1.5),
        "matrices": draw_matrices(jax.random.fold_in(splits[7], 71), 0),
        "gain_momentum": scatter_about(splits[5], (2, D), 0.05, 0.3, ((1, 8),), jnp.float32),
        "mat_momentum": scatter_about(splits[6], (D, 4 * FF), 0.02, 0.12, ((0, 8),), jnp.float32),
    }


HIGH = lax.Precision.HIGHEST
EPS_NORM = 1e-05
ROPE_BASE = 100000.0
MOMENT = 0.95
LEARN = 0.05
GAIN_LEARN = 0.1
COEF_A = 3.4445
COEF_B = -4.775
COEF_C = 2.0315

@jax.custom_vjp
def low(v):
    return lax.optimization_barrier(v.astype(jnp.bfloat16)).astype(jnp.float32)

@jax.custom_vjp
def low_back(v):
    return v

def low_keep(v):
    return (low(v), None)

def low_pass(kept, grad):
    return (grad,)

def back_keep(v):
    return (v, None)

def back_low(kept, grad):
    return (low(grad),)
low.defvjp(low_keep, low_pass)
low_back.defvjp(back_keep, back_low)

def matmul(left, right):
    return jnp.dot(left, right, precision=HIGH)

def rms_unit(values):
    return values * lax.rsqrt(lax.optimization_barrier(jnp.mean(values * values, axis=-1, keepdims=True)) + EPS_NORM)

def rope_tables(segment):
    seq_len = segment.shape[0]
    token_index = jnp.arange(seq_len, dtype=jnp.int32)
    first_mark = jnp.concatenate([jnp.ones((1,), dtype=bool), segment[1:] != segment[:-1]])
    start_index = lax.cummax(jnp.where(first_mark, token_index, 0), axis=0)
    offset = (token_index - start_index).astype(jnp.float32)
    inverse = 1.0 / ROPE_BASE ** (jnp.arange(0, HD, 2, dtype=jnp.float32) / HD)
    angle = offset[:, None] * inverse[None, :]
    return (jnp.cos(angle)[:, None, :], jnp.sin(angle)[:, None, :])

def rotate(values, cosine, sine):
    half_dim = values.shape[-1] // 2
    first_half = values[..., :half_dim]
    second_half = values[..., half_dim:]
    return jnp.concatenate([first_half * cosine - second_half * sine, second_half * cosine + first_half * sine], axis=-1)

def layer(inputs, segment, gain_pair, weights):
    seq_len = inputs.shape[0]
    kv_cols = KVH * HD
    group_size = HEADS // KVH
    gain_low = low(gain_pair)
    weight_low = low(weights)
    cosine, sine = rope_tables(segment)
    normed = low(rms_unit(inputs) * gain_low[0])
    query_p = low_back(matmul(normed, weight_low[:, :D]))
    key_p = low_back(matmul(normed, weight_low[:, D:D + kv_cols]))
    value_p = low(low_back(matmul(normed, weight_low[:, D + kv_cols:D + 2 * kv_cols])))
    query_r = low(rotate(query_p.reshape(seq_len, HEADS, HD), cosine, sine)).reshape(seq_len, KVH, group_size, HD)
    key_r = low(rotate(key_p.reshape(seq_len, KVH, HD), cosine, sine))
    scores = jnp.einsum('qkgd,tkd->kgqt', query_r, key_r, precision=HIGH) * 0.125
    scores = low_back(scores)
    token_index = jnp.arange(seq_len, dtype=jnp.int32)
    allowed = (token_index[None, :] <= token_index[:, None]) & (segment[None, :] == segment[:, None])
    scores = jnp.where(allowed, scores, -1e+30)
    row_max = lax.optimization_barrier(jnp.max(scores, axis=-1, keepdims=True))
    exponent = jnp.exp(scores - row_max)
    attention_p = low(exponent / lax.optimization_barrier(jnp.sum(exponent, axis=-1, keepdims=True)))
    mixed_heads = jnp.einsum('kgqt,tkd->qkgd', attention_p, value_p.reshape(seq_len, KVH, HD), precision=HIGH).reshape(seq_len, D)
    mixed_heads = low(low_back(mixed_heads))
    middle = inputs + low_back(matmul(mixed_heads, weight_low[:, D + 2 * kv_cols:FF]))
    normed_two = low(rms_unit(middle) * gain_low[1])
    gate_pre = low_back(matmul(normed_two, weight_low[:, FF:2 * FF]))
    up_pre = low_back(matmul(normed_two, weight_low[:, 2 * FF:3 * FF]))
    inner_act = low(jax.nn.silu(gate_pre) * up_pre)
    branch = low_back(lax.dot_general(inner_act, weight_low[:, 3 * FF:], (((1,), (1,)), ((), ())), precision=HIGH))
    return middle + branch

def orthogonal(matrix):
    tall = matrix.shape[0] > matrix.shape[1]
    work = matrix.T if tall else matrix
    work = work / (jnp.sqrt(jnp.sum(work * work)) + 1e-07)
    for sweep_id in range(NS_STEPS):
        gram = jnp.dot(work, work.T, precision=HIGH)
        poly = COEF_B * gram + COEF_C * jnp.dot(gram, gram, precision=HIGH)
        work = COEF_A * work + jnp.dot(poly, work, precision=HIGH)
    if tall:
        work = work.T
    return work * (0.2 * math.sqrt(max(matrix.shape)))

def orthogonalize_all(look):
    kv_cols = KVH * HD
    bounds = [0, D, D + kv_cols, D + 2 * kv_cols, FF, 2 * FF, 3 * FF, 4 * FF]
    pieces = [orthogonal(look[:, bounds[block_id]:bounds[block_id + 1]]) for block_id in range(7)]
    return jnp.concatenate(pieces, axis=1)

def reference(hidden_in, seg_ids, out_grad, gains, matrices, gain_momentum, mat_momentum):
    seq_total = MB * SEQS
    inputs_all = hidden_in.reshape(seq_total, SEQ, D)
    segments_all = seg_ids.reshape(seq_total, SEQ)
    cotangents = out_grad.reshape(seq_total, SEQ, D)

    def one_sequence(running, element):
        inputs, segment, cotangent = element

        def forward(values, gain_pair, weights):
            return layer(values, segment, gain_pair, weights)
        output, pullback = jax.vjp(forward, inputs.astype(jnp.float32), gains, matrices)
        d_input, d_gains, d_weights = pullback(cotangent.astype(jnp.float32))
        return ((running[0] + d_gains, running[1] + d_weights), (output.astype(jnp.bfloat16), d_input))
    start_acc = (jnp.zeros((2, D), jnp.float32), jnp.zeros((D, 4 * FF), jnp.float32))
    totals, outputs = lax.scan(one_sequence, start_acc, (inputs_all, segments_all, cotangents))
    grad_scale = TOKENS ** (-0.5)
    gain_grad = totals[0] * grad_scale
    matrix_grad = totals[1] * grad_scale
    new_mat_momentum = MOMENT * mat_momentum + matrix_grad
    new_gain_momentum = MOMENT * gain_momentum + gain_grad
    look = matrix_grad + MOMENT * new_mat_momentum
    new_matrices = matrices - LEARN * orthogonalize_all(look)
    spread = lax.rsqrt(lax.optimization_barrier(jnp.mean(new_gain_momentum * new_gain_momentum, axis=1, keepdims=True)) + 1e-06)
    new_gains = gains - GAIN_LEARN * new_gain_momentum * spread
    out_hidden = outputs[0].reshape(MB, SEQS, SEQ, D)
    in_grad = outputs[1].reshape(MB, SEQS, SEQ, D)
    return (out_hidden, in_grad, matrix_grad, gain_grad, new_mat_momentum, new_gain_momentum, new_matrices, new_gains)
```

```python
import functools
import math

import jax
import jax.numpy as jnp
from jax import lax
from jax.experimental import pallas as pl
from jax.experimental.pallas import tpu as pltpu
from jax.sharding import PartitionSpec as P

D = 576
HEADS = 9
KVH = 3
HD = 64
FF = 1536
KV = KVH * HD
QKV = D + 2 * KV
NS_STEPS = 5
WINDOW = 512
SEGMENTS = 8

EPS_NORM = 1e-05
ROPE_BASE = 100000.0
MOMENT = 0.95
LEARN = 0.05
GAIN_LEARN = 0.1
COEF_A = 3.4445
COEF_B = -4.775
COEF_C = 2.0315
F32 = jnp.float32
BF16 = jnp.bfloat16
TQ = 256
TM = 512
FC = 512
VMEM_LIMIT = 60 * 1024 * 1024


def dot(a, b):
    return jnp.dot(a, b, preferred_element_type=F32)


def dot_nt(a, b):
    return lax.dot_general(a, b, (((1,), (1,)), ((), ())), preferred_element_type=F32)


def dot_tn(a, b):
    return lax.dot_general(a, b, (((0,), (0,)), ((), ())), preferred_element_type=F32)


def lane_iota(rows):
    return lax.broadcasted_iota(jnp.int32, (rows, 128), 1)


def swap_pairs(z, lane):
    return jnp.where(lane % 64 < 32, pltpu.roll(z, 96, 1), pltpu.roll(z, 32, 1))


def key_span(tile):
    first = max(0, (tile * TQ - (WINDOW - 1)) // TQ * TQ)
    return first, (tile + 1) * TQ


def mask_bias(start_ref, tile):
    first, stop = key_span(tile)
    width = stop - first
    query = tile * TQ + lax.broadcasted_iota(jnp.int32, (TQ, width), 0)
    key = first + lax.broadcasted_iota(jnp.int32, (TQ, width), 1)
    start = start_ref[tile * TQ : (tile + 1) * TQ, :]
    return jnp.where((key <= query) & (key >= start), 0.0, -1e30).astype(F32)


def place_heads(chunk, lane, take_low):
    other = pltpu.roll(chunk, 64, 1)
    low = chunk if take_low else other
    high = other if take_low else chunk
    return (
        jnp.where(lane < 64, low, 0.0).astype(BF16),
        jnp.where(lane < 64, 0.0, high).astype(BF16),
    )


def place_keys(chunks, lane, kz_ref, vz_ref, rows):
    spots = [(4, False), (5, True), (5, False)], [(6, True), (6, False), (7, True)]
    for ref, spot in zip((kz_ref, vz_ref), spots):
        for head, (chunk, take_low) in enumerate(spot):
            low, high = place_heads(chunks[chunk], lane, take_low)
            ref[0, head, rows, :] = low
            ref[1, head, rows, :] = high


def norm_rows(values):
    return lax.rsqrt(jnp.mean(values * values, axis=-1, keepdims=True) + EPS_NORM)


def attention_fwd_kernel(
    x_ref, cos_ref, sin_ref, start_ref, g1_ref, w_ref, qkv_ref, o_ref, lse_ref, kz_ref, vz_ref
):
    seq = x_ref.shape[0]
    lane = lane_iota(TQ)
    for tile in range(seq // TQ):
        rows = slice(tile * TQ, (tile + 1) * TQ)
        x = x_ref[rows, :].astype(F32)
        a = (x * norm_rows(x) * g1_ref[...]).astype(BF16)
        proj = dot(a, w_ref[...])
        cos, sin = cos_ref[rows, :], sin_ref[rows, :]
        chunks = {}
        for c in range(8):
            z = proj[:, c * 128 : min((c + 1) * 128, QKV)]
            if c == 7:
                z = jnp.concatenate([z, z], axis=1)
            if c < 6:
                z = z * cos + swap_pairs(z, lane) * sin
            if c < 4:
                z = z * 0.125
            if c == 4:
                z = jnp.where(lane < 64, z * 0.125, z)
            chunks[c] = z
            low = z.astype(BF16)
            if c < 7:
                qkv_ref[rows, c * 128 : (c + 1) * 128] = low
            else:
                qkv_ref[rows, c * 128 : QKV] = low[:, :64]
        place_keys(chunks, lane, kz_ref, vz_ref, rows)
    for tile in range(seq // TQ):
        rows = slice(tile * TQ, (tile + 1) * TQ)
        first, stop = key_span(tile)
        bias = mask_bias(start_ref, tile)
        lse = jnp.zeros((TQ, 128), F32)
        for c in range(5):
            q = qkv_ref[rows, c * 128 : (c + 1) * 128]
            out = None
            for half in range(2 if c < 4 else 1):
                head = 2 * c + half
                group = head // (HEADS // KVH)
                s = dot_nt(q, kz_ref[half, group, first:stop, :]) + bias
                top = jnp.max(s, axis=-1, keepdims=True)
                e = jnp.exp(s - top)
                total = jnp.sum(e, axis=-1, keepdims=True)
                p = (e * (1.0 / total)).astype(BF16)
                part = dot(p, vz_ref[half, group, first:stop, :])
                out = part if out is None else out + part
                lse = jnp.where(lane == head, top + jnp.log(total), lse)
            if c < 4:
                o_ref[rows, c * 128 : (c + 1) * 128] = out.astype(BF16)
            else:
                o_ref[rows, c * 128 : D] = out[:, :64].astype(BF16)
        lse_ref[rows, :] = lse


def feed_kernel(
    x_ref, o_ref, dy_ref, g2_ref, wo_ref, wg_ref, wu_ref, wd_ref,
    out_ref, dh2_ref, do_ref, go_ref, gg_ref, gu_ref, gd_ref, dg2_ref,
    acc_o, acc_g, acc_u, acc_d,
):
    step = pl.program_id(0)

    @pl.when(step == 0)
    def _():
        acc_o[...] = jnp.zeros_like(acc_o)
        acc_g[...] = jnp.zeros_like(acc_g)
        acc_u[...] = jnp.zeros_like(acc_u)
        acc_d[...] = jnp.zeros_like(acc_d)
        dg2_ref[...] = jnp.zeros_like(dg2_ref)

    g2 = g2_ref[...]
    o = o_ref[...]
    h2 = x_ref[...].astype(F32) + dot(o, wo_ref[...])
    r2 = norm_rows(h2)
    u2 = h2 * r2
    b = (u2 * g2).astype(BF16)
    dm = dy_ref[...]
    result = h2
    db = jnp.zeros_like(h2)
    for c in range(FF // FC):
        cols = slice(c * FC, (c + 1) * FC)
        wg, wu, wd = wg_ref[:, cols], wu_ref[:, cols], wd_ref[:, cols]
        gate = dot(b, wg)
        up = dot(b, wu)
        dinner = dot(dm, wd)
        sig = 0.5 + 0.5 * jnp.tanh(0.5 * gate)
        silu = gate * sig
        inner = (silu * up).astype(BF16)
        dgate = (dinner * up * (sig + silu * (1.0 - sig))).astype(BF16)
        dup = (dinner * silu).astype(BF16)
        result = result + dot_nt(inner, wd)
        acc_d[:, cols] += dot_tn(dm, inner)
        db = db + dot_nt(dgate, wg) + dot_nt(dup, wu)
        acc_g[:, cols] += dot_tn(b, dgate)
        acc_u[:, cols] += dot_tn(b, dup)
    out_ref[...] = result.astype(BF16)
    dg2_ref[...] += jnp.sum(db * u2, axis=0, keepdims=True)
    e2 = db * g2
    dh2 = r2 * (e2 - u2 * jnp.mean(e2 * u2, axis=-1, keepdims=True)) + dm.astype(F32)
    dh2_ref[...] = dh2
    dattn = dh2.astype(BF16)
    acc_o[...] += dot_tn(o, dattn)
    do_ref[...] = dot_nt(dattn, wo_ref[...]).astype(BF16)

    @pl.when(step == pl.num_programs(0) - 1)
    def _():
        go_ref[...] = acc_o[...].astype(BF16)
        gg_ref[...] = acc_g[...].astype(BF16)
        gu_ref[...] = acc_u[...].astype(BF16)
        gd_ref[...] = acc_d[...].astype(BF16)


def attention_bwd_kernel(
    x_ref, cos_ref, sin_ref, start_ref, g1_ref, w_ref, qkv_ref, o_ref, lse_ref, do_ref, dh2_ref,
    dx_ref, gq_ref, dg1_ref,
    kz_ref, vz_ref, kvt_ref, dq_ref, acc,
):
    seq = x_ref.shape[0]
    lane = lane_iota(TQ)

    @pl.when(pl.program_id(0) == 0)
    def _():
        acc[...] = jnp.zeros_like(acc)
        dg1_ref[...] = jnp.zeros_like(dg1_ref)

    for tile in range(seq // TQ):
        rows = slice(tile * TQ, (tile + 1) * TQ)
        chunks = {}
        for c in range(4, 8):
            z = qkv_ref[rows, c * 128 : min((c + 1) * 128, QKV)].astype(F32)
            if c == 7:
                z = jnp.concatenate([z, z], axis=1)
            chunks[c] = z
        place_keys(chunks, lane, kz_ref, vz_ref, rows)
    kvt_ref[...] = jnp.zeros_like(kvt_ref)
    for tile in range(seq // TQ):
        rows = slice(tile * TQ, (tile + 1) * TQ)
        first, stop = key_span(tile)
        bias = mask_bias(start_ref, tile)
        lse = lse_ref[rows, :]
        cos, sin = cos_ref[rows, :], sin_ref[rows, :]
        for c in range(5):
            wide = slice(c * 128, (c + 1) * 128)
            q = qkv_ref[rows, wide]
            if c < 4:
                do = do_ref[rows, wide]
                o = o_ref[rows, wide]
            else:
                do = do_ref[rows, c * 128 : D]
                do = jnp.concatenate([do, do], axis=1)
                o = o_ref[rows, c * 128 : D]
                o = jnp.concatenate([o, o], axis=1)
            prod = do.astype(F32) * o.astype(F32)
            dq = None
            for half in range(2 if c < 4 else 1):
                head = 2 * c + half
                group = head // (HEADS // KVH)
                mine = lane < 64 if half == 0 else lane >= 64
                delta = jnp.sum(jnp.where(mine, prod, 0.0), axis=-1, keepdims=True)
                kz = kz_ref[half, group, first:stop, :]
                s = dot_nt(q, kz) + bias
                p = jnp.exp(s - lse[:, head : head + 1])
                dp = dot_nt(do, vz_ref[half, group, first:stop, :])
                ds = (p * (dp - delta)).astype(BF16)
                pl_ = p.astype(BF16)
                part = dot(ds, kz)
                dq = part if dq is None else dq + part
                own = slice(half * 64, half * 64 + 64)
                krow = 64 + group * 64
                vrow = 256 + group * 64
                kvt_ref[krow : krow + 64, first:stop] += dot_tn(q, ds)[own, :]
                kvt_ref[vrow : vrow + 64, first:stop] += dot_tn(do, pl_)[own, :]
            dq = dq * 0.125
            dq = dq * cos - swap_pairs(dq, lane) * sin
            dq_ref[rows, wide] = dq.astype(BF16)
    for tile in range(seq // TQ):
        rows = slice(tile * TQ, (tile + 1) * TQ)
        cos, sin = cos_ref[rows, :], sin_ref[rows, :]
        for c in range(4):
            z = kvt_ref[c * 128 : (c + 1) * 128, rows].T
            if c < 2:
                z = z * cos - swap_pairs(z, lane) * sin
            z = z.astype(BF16)
            if c == 0:
                z = jnp.where(lane < 64, dq_ref[rows, 512:640].astype(F32), z.astype(F32)).astype(BF16)
            wide = slice(512 + c * 128, 512 + (c + 1) * 128)
            dq_ref[rows, wide] = z
        x = x_ref[rows, :].astype(F32)
        g1 = g1_ref[...]
        r1 = norm_rows(x)
        u1 = x * r1
        a = (u1 * g1).astype(BF16)
        dqkv = dq_ref[rows, 0:QKV]
        acc[...] += dot_tn(a, dqkv)
        da = dot_nt(dqkv, w_ref[...])
        dg1_ref[...] += jnp.sum(da * u1, axis=0, keepdims=True)
        e1 = da * g1
        dx_ref[rows, :] = r1 * (e1 - u1 * jnp.mean(e1 * u1, axis=-1, keepdims=True)) + dh2_ref[rows, :]

    @pl.when(pl.program_id(0) == pl.num_programs(0) - 1)
    def _():
        gq_ref[...] = acc[...].astype(BF16)


def whole(shape):
    zeros = (0,) * len(shape)
    return pl.BlockSpec(shape, lambda *_: zeros, pipeline_mode=pl.Buffered(1))


def per_seq(width, seq):
    return pl.BlockSpec((None, seq, width), lambda s: (s, 0, 0))


def attention_fwd(x, cos, sin, start, g1, w):
    count, seq, _ = x.shape
    return pl.pallas_call(
        attention_fwd_kernel,
        grid=(count,),
        in_specs=[
            per_seq(D, seq), per_seq(128, seq), per_seq(128, seq), per_seq(1, seq),
            whole((1, D)), whole((D, QKV)),
        ],
        out_specs=[per_seq(QKV, seq), per_seq(D, seq), per_seq(128, seq)],
        out_shape=[
            jax.ShapeDtypeStruct((count, seq, QKV), BF16),
            jax.ShapeDtypeStruct((count, seq, D), BF16),
            jax.ShapeDtypeStruct((count, seq, 128), F32),
        ],
        scratch_shapes=[
            pltpu.VMEM((2, KVH, seq, 128), BF16),
            pltpu.VMEM((2, KVH, seq, 128), BF16),
        ],
        compiler_params=pltpu.CompilerParams(vmem_limit_bytes=VMEM_LIMIT),
        cost_estimate=pl.CostEstimate(
            flops=count * 30_000_000_000, bytes_accessed=count * 10_000_000, transcendentals=0
        ),
        name="attention_fwd",
    )(x, cos, sin, start, g1, w)


def feed(x, o, dy, g2, wo, wg, wu, wd):
    tokens = x.shape[0]
    tile = min(TM, tokens)

    def rows(width):
        return pl.BlockSpec((tile, width), lambda t: (t, 0))

    return pl.pallas_call(
        feed_kernel,
        grid=(tokens // tile,),
        in_specs=[rows(D), rows(D), rows(D), whole((1, D)), whole((D, D))]
        + [whole((D, FF))] * 3,
        out_specs=[rows(D), rows(D), rows(D), whole((D, D))] + [whole((D, FF))] * 3 + [whole((1, D))],
        out_shape=[
            jax.ShapeDtypeStruct((tokens, D), BF16),
            jax.ShapeDtypeStruct((tokens, D), F32),
            jax.ShapeDtypeStruct((tokens, D), BF16),
            jax.ShapeDtypeStruct((D, D), BF16),
            jax.ShapeDtypeStruct((D, FF), BF16),
            jax.ShapeDtypeStruct((D, FF), BF16),
            jax.ShapeDtypeStruct((D, FF), BF16),
            jax.ShapeDtypeStruct((1, D), F32),
        ],
        scratch_shapes=[pltpu.VMEM((D, D), F32)] + [pltpu.VMEM((D, FF), F32)] * 3,
        compiler_params=pltpu.CompilerParams(vmem_limit_bytes=VMEM_LIMIT),
        cost_estimate=pl.CostEstimate(
            flops=tokens * 18_000_000, bytes_accessed=30_000_000, transcendentals=0
        ),
        name="feed",
    )(x, o, dy, g2, wo, wg, wu, wd)


def attention_bwd(x, cos, sin, start, g1, w, qkv, o, lse, do, dh2):
    count, seq, _ = x.shape
    return pl.pallas_call(
        attention_bwd_kernel,
        grid=(count,),
        in_specs=[
            per_seq(D, seq), per_seq(128, seq), per_seq(128, seq), per_seq(1, seq),
            whole((1, D)), whole((D, QKV)),
            per_seq(QKV, seq), per_seq(D, seq), per_seq(128, seq), per_seq(D, seq), per_seq(D, seq),
        ],
        out_specs=[per_seq(D, seq), whole((D, QKV)), whole((1, D))],
        out_shape=[
            jax.ShapeDtypeStruct((count, seq, D), F32),
            jax.ShapeDtypeStruct((D, QKV), BF16),
            jax.ShapeDtypeStruct((1, D), F32),
        ],
        scratch_shapes=[
            pltpu.VMEM((2, KVH, seq, 128), BF16),
            pltpu.VMEM((2, KVH, seq, 128), BF16),
            pltpu.VMEM((512, seq), F32),
            pltpu.VMEM((seq, 1024), BF16),
            pltpu.VMEM((D, QKV), F32),
        ],
        compiler_params=pltpu.CompilerParams(vmem_limit_bytes=VMEM_LIMIT),
        cost_estimate=pl.CostEstimate(
            flops=count * 50_000_000_000, bytes_accessed=count * 12_000_000, transcendentals=0
        ),
        name="attention_bwd",
    )(x, cos, sin, start, g1, w, qkv, o, lse, do, dh2)


def sweep(work, scale, shift):
    low = work.astype(BF16)
    size = work.shape[0]
    gram = dot_nt(low, low)
    if shift:
        eye = lax.broadcasted_iota(jnp.int32, (size, size), 0) == lax.broadcasted_iota(
            jnp.int32, (size, size), 1
        )
        gram = gram - jnp.where(eye, shift, 0.0)
    glow = gram.astype(BF16)
    poly = (COEF_B + 2 * COEF_C * shift) * gram + COEF_C * dot(glow, glow)
    return (COEF_A + COEF_B * shift + COEF_C * shift * shift) * work + dot(poly.astype(BF16), low)


def orthogonalize_kernel(shifts, scale, x_ref, out_ref):
    work = x_ref[...].astype(F32)
    work = work * (1.0 / (jnp.sqrt(jnp.sum(work * work)) + 1e-07))
    out_ref[...] = work
    for shift in shifts:
        out_ref[...] = sweep(out_ref[...], scale, shift)
    out_ref[...] = out_ref[...] * scale


def orthogonalize(block):
    rows, cols = block.shape
    if rows > cols:
        return orthogonalize(block.T).T
    shifts = (0.0, 0.0, 0.8, 0.8, 0.8) if rows <= 256 else (0.0, 0.0, 0.0, 0.8, 0.8)
    return pl.pallas_call(
        functools.partial(orthogonalize_kernel, shifts, 0.2 * math.sqrt(max(rows, cols))),
        out_shape=jax.ShapeDtypeStruct((rows, cols), F32),
        compiler_params=pltpu.CompilerParams(vmem_limit_bytes=VMEM_LIMIT),
        name="orthogonalize",
    )(block)


def attention_block(block):
    bounds = [0, D, D + KV, D + 2 * KV, FF]
    pieces = [orthogonalize(block[:, bounds[i] : bounds[i + 1]]) for i in range(4)]
    return jnp.concatenate(pieces, axis=1)


def rope_tables(seg):
    count, seq = seg.shape
    start = jnp.zeros_like(seg)
    for value in range(1, SEGMENTS):
        before = jnp.sum((seg < value).astype(jnp.int32), axis=1, keepdims=True)
        start = jnp.where(seg == value, before, start)
    offset = (jnp.arange(seq, dtype=jnp.int32)[None, :] - start).astype(F32)
    inverse = 1.0 / ROPE_BASE ** (jnp.arange(0, HD, 2, dtype=F32) / HD)
    angle = offset[:, :, None] * inverse[None, None, :]
    cos, sin = jnp.cos(angle), jnp.sin(angle)
    return (
        start[:, :, None],
        jnp.concatenate([cos, cos, cos, cos], axis=-1),
        jnp.concatenate([-sin, sin, -sin, sin], axis=-1),
    )


def layer_pass(x, seg, dy, gains, w_qkv, w_o, w_g, w_u, w_d):
    count, seq, _ = x.shape
    start, cos, sin = rope_tables(seg)
    g1, g2 = gains[0:1], gains[1:2]
    qkv, o, lse = attention_fwd(x, cos, sin, start, g1, w_qkv)
    flat = lambda v: v.reshape(count * seq, v.shape[-1])
    deep = lambda v: v.reshape(count, seq, v.shape[-1])
    out, dh2, do, go, gg, gu, gd, dg2 = feed(flat(x), flat(o), flat(dy), g2, w_o, w_g, w_u, w_d)
    dx, gq, dg1 = attention_bwd(x, cos, sin, start, g1, w_qkv, qkv, o, lse, deep(do), deep(dh2))
    return deep(out), dx, (gq, go, gg, gu, gd), jnp.concatenate([dg1, dg2], axis=0)


def on_device(hidden_in, seg_ids, out_grad, gains, matrices, gain_momentum, mat_momentum):
    shard_rows = matrices.shape[0]
    total_cols = matrices.shape[1]
    count, local, seq, _ = hidden_in.shape
    total_tokens = count * local * seq * lax.axis_size("dp") * lax.axis_size("fsdp")
    grad_scale = float(total_tokens) ** (-0.5)
    shard_low = matrices.astype(BF16)
    cuts = [0, QKV, FF, 2 * FF, 3 * FF, 4 * FF]
    gather = lambda v: lax.all_gather(v, "fsdp", axis=0, tiled=True)
    w_qkv = gather(shard_low[:, :QKV])
    gain_pair = gather(gains.T.astype(BF16)).astype(F32).T
    w_o = gather(shard_low[:, QKV:FF])
    w_g, w_u, w_d = (gather(shard_low[:, cuts[i] : cuts[i + 1]]) for i in (2, 3, 4))
    x = hidden_in.reshape(count * local, seq, D)
    dy = out_grad.reshape(count * local, seq, D)
    seg = seg_ids.reshape(count * local, seq)
    out, dx, grads, gain_grads = layer_pass(x, seg, dy, gain_pair, w_qkv, w_o, w_g, w_u, w_d)
    shards = [lax.psum_scatter(g, "fsdp", scatter_dimension=0, tiled=True) for g in grads]
    summed = lax.psum(jnp.concatenate(shards, axis=1).astype(F32), "dp")
    summed_gains = lax.psum(
        lax.psum_scatter(gain_grads.T, "fsdp", scatter_dimension=0, tiled=True), "dp"
    )
    matrix_grad = summed * grad_scale
    gain_grad = (summed_gains * grad_scale).T
    new_mat_momentum = MOMENT * mat_momentum + matrix_grad
    new_gain_momentum = MOMENT * gain_momentum + gain_grad
    look = matrix_grad + MOMENT * new_mat_momentum
    owner_group = lax.axis_index("dp")
    block_cols = total_cols // 4
    own_block = lax.dynamic_slice_in_dim(look, owner_group * block_cols, block_cols, 1)
    whole_block = gather(own_block.astype(BF16))
    whole_gain_mom = gather(new_gain_momentum.T)
    orthogonal_block = lax.cond(owner_group == 0, attention_block, orthogonalize, whole_block)
    own_rows = lax.dynamic_slice_in_dim(
        orthogonal_block, lax.axis_index("fsdp") * shard_rows, shard_rows, 0
    )
    update_rows = lax.all_gather(own_rows.astype(BF16), "dp", axis=1, tiled=True).astype(F32)
    new_matrices = matrices - LEARN * update_rows
    spread = lax.rsqrt(jnp.mean(whole_gain_mom * whole_gain_mom, axis=0, keepdims=True) + 1e-06)
    new_gains = gains - GAIN_LEARN * new_gain_momentum * spread.T
    return (
        out.reshape(hidden_in.shape),
        dx.reshape(hidden_in.shape),
        matrix_grad,
        gain_grad,
        new_mat_momentum,
        new_gain_momentum,
        new_matrices,
        new_gains,
    )


def solution(mesh):
    in_specs = (
        P(None, ("dp", "fsdp"), None, None),
        P(None, ("dp", "fsdp"), None),
        P(None, ("dp", "fsdp"), None, None),
        P(None, "fsdp"),
        P("fsdp", None),
        P(None, "fsdp"),
        P("fsdp", None),
    )
    out_specs = (
        P(None, ("dp", "fsdp"), None, None),
        P(None, ("dp", "fsdp"), None, None),
        P("fsdp", None),
        P(None, "fsdp"),
        P("fsdp", None),
        P(None, "fsdp"),
        P("fsdp", None),
        P(None, "fsdp"),
    )
    return jax.shard_map(
        on_device, mesh=mesh, in_specs=in_specs, out_specs=out_specs, check_vma=False
    )
```
